32 devices in a mesh: band: 4 (over y, x), slab: 8 (over z, core).
Axes of the slice: x: 2, y: 2, z: 4, core: 2. Of those that a mesh axis runs over, the one named last changes fastest.
Arguments:
- band_block: float32 [4, 2, 2, 128, 128, 128], P(None, None, None, 'band', 'slab'), may hold values from -24 to 24
- material_grid: int32 [128, 128, 128], P('slab'), may hold values from 0 to 3
- inverse_permittivity: float32 [4], replicated, may hold values from 0.077 to 1
- bloch_index: int32 [1], replicated, may hold values from 0 to 7
Outputs:
- search_block: float32 [4, 2, 2, 128, 128, 128], P(None, None, None, 'band', 'slab')
- correlation: float32 [2, 8, 8], replicated
- projected: float32 [2, 8, 8], replicated
The draws below stay inside these ranges and needn't reach their ends.
All inputs are finite; a program needn't handle non-finite values.
Results may differ from the reference program's by a relative error of at most 0.00005.
Values sent between devices are 32-bit elements; how exact they have to be, the bound alone decides.
A program may use at most 192 MiB of HBM per device.

```python
import math
import jax
import jax.numpy as jnp
from jax import lax

NX = 128
NY = 128
NZ = 128
MATERIALS = 4
KPOINTS = 8
BANDS = 4
NPTS = 2097152


def signed_fraction(length):
    indices = jnp.arange(length, dtype=jnp.int32)
    signed = jnp.where(indices >= length // 2, indices - length, indices).astype(jnp.float32)
    return signed / length


def draw_band_block(key, part):
    own_key = jax.random.fold_in(key, 11)
    common_key = jax.random.fold_in(key, 12)
    grid_shape = (BANDS, 2, 2, NZ, NY, NX)
    common = jnp.clip(jax.random.normal(common_key, (1, 2, 2, NZ, NY, NX), jnp.float32), -4.0, 4.0)
    own = jnp.clip(jax.random.normal(own_key, grid_shape, jnp.float32), -4.0, 4.0)
    depth_part = signed_fraction(NZ)[:, None, None]
    height_part = signed_fraction(NY)[None, :, None]
    width_part = signed_fraction(NX)[None, None, :]
    envelope = 3.0 / (1.0 + 12.0 * (depth_part * depth_part + height_part * height_part + width_part * width_part))
    return (envelope * (own + 0.7 * common)).astype(jnp.float32)


def set_ends(drawn, key, smallest, largest):
    index_at = [jax.random.randint(jax.random.fold_in(key, axis), (), 0, length) for axis, length in enumerate(drawn.shape)]
    longest = drawn.shape.index(max(drawn.shape))
    next_to = index_at[:longest] + [(index_at[longest] + 1) % drawn.shape[longest]] + index_at[longest + 1:]
    return drawn.at[tuple(index_at)].set(smallest).at[tuple(next_to)].set(largest)


def setup_inputs(seed: int = 0) -> dict:
    key_list = jax.random.split(jax.random.key(seed), 5)
    band_block = draw_band_block(jax.random.fold_in(key_list[4], 71), 0)
    material_grid = set_ends(jax.random.randint(key_list[1], (NZ, NY, NX), 0, MATERIALS), jax.random.fold_in(key_list[1], 1), 0, MATERIALS - 1).astype(jnp.int32)
    inverse_permittivity = jnp.clip(jnp.exp(jax.random.uniform(key_list[2], (MATERIALS,), jnp.float32, math.log(0.077), math.log(1.0))), 0.077, 1.0)
    bloch_index = jax.random.randint(key_list[3], (1,), 0, KPOINTS).astype(jnp.int32)
    return dict(band_block=band_block, material_grid=material_grid, inverse_permittivity=inverse_permittivity, bloch_index=bloch_index)


HIGHEST = lax.Precision.HIGHEST

def axis_values(length, weight, fraction, offset, extent):
    indices = offset + jnp.arange(extent, dtype=jnp.int32)
    signed = jnp.where(indices >= length // 2, indices - length, indices).astype(jnp.float32)
    return 2.0 * math.pi / length * (signed + weight * fraction)

def frame(depth_wave, height_wave, width_wave):
    depth_term = depth_wave[:, None, None]
    height_term = height_wave[None, :, None]
    width_term = width_wave[None, None, :]
    planar = jnp.sqrt(width_term * width_term + height_term * height_term)
    magnitude = jnp.sqrt(planar * planar + depth_term * depth_term)
    grid_shape = magnitude.shape
    primary = [jnp.broadcast_to(height_term / planar, grid_shape), jnp.broadcast_to(-width_term / planar, grid_shape), jnp.zeros(grid_shape, magnitude.dtype)]
    secondary = [width_term * depth_term / (magnitude * planar), height_term * depth_term / (magnitude * planar), jnp.broadcast_to(-planar / magnitude, grid_shape)]
    return (primary, secondary, magnitude)

def curl_field(block, primary, secondary, magnitude):
    first_comp = block[:, 0]
    second_comp = block[:, 1]
    parts = [magnitude * (first_comp * secondary[component] - second_comp * primary[component]) for component in range(3)]
    return jnp.stack(parts, axis=1).reshape((-1,) + first_comp.shape[1:])

def project_back(spectrum, primary, secondary, magnitude, band_count):
    grouped = spectrum.reshape((band_count, 3) + spectrum.shape[1:])
    along_second = grouped[:, 0] * secondary[0] + grouped[:, 1] * secondary[1] + grouped[:, 2] * secondary[2]
    along_primary = grouped[:, 0] * primary[0] + grouped[:, 1] * primary[1] + grouped[:, 2] * primary[2]
    return jnp.stack([magnitude * along_second, -magnitude * along_primary], axis=1)

def operate(block, inverse_cells, primary, secondary, magnitude):

    def one_band(single):
        curled = curl_field(single[None], primary, secondary, magnitude)
        spectrum = curled[:, 0] + 1j * curled[:, 1]
        spatial = jnp.fft.ifftn(spectrum, axes=(1, 2, 3)) * inverse_cells
        returned = jnp.fft.fftn(spatial, axes=(1, 2, 3))
        values = jnp.stack([jnp.real(returned), jnp.imag(returned)], axis=1)
        return project_back(values, primary, secondary, magnitude, 1)[0]
    return lax.map(one_band, block)

def gram_parts(left, right):
    left_real = left[:, :, 0].reshape(left.shape[0], -1)
    left_imag = left[:, :, 1].reshape(left.shape[0], -1)
    right_real = right[:, :, 0].reshape(right.shape[0], -1)
    right_imag = right[:, :, 1].reshape(right.shape[0], -1)
    inner_product = lambda first_rows, second_rows: jnp.einsum('km,jm->kj', first_rows, second_rows, precision=HIGHEST)
    real_sum = inner_product(left_real, right_real) + inner_product(left_imag, right_imag)
    imag_sum = inner_product(left_real, right_imag) - inner_product(left_imag, right_real)
    return (real_sum / NPTS, imag_sum / NPTS)

def reference(band_block, material_grid, inverse_permittivity, bloch_index):
    fraction = (bloch_index[0].astype(jnp.float32) + 1.0) / KPOINTS
    primary, secondary, magnitude = frame(axis_values(NZ, 0.2, fraction, 0, NZ), axis_values(NY, 0.35, fraction, 0, NY), axis_values(NX, 0.5, fraction, 0, NX))
    inverse_cells = inverse_permittivity[material_grid]
    image = operate(band_block, inverse_cells, primary, secondary, magnitude)
    correlation_real, correlation_imag = gram_parts(band_block, band_block)
    cross_real, cross_imag = gram_parts(band_block, image)
    system = jnp.concatenate([jnp.concatenate([correlation_real, -correlation_imag], 1), jnp.concatenate([correlation_imag, correlation_real], 1)], 0)
    right_side = jnp.concatenate([cross_real, cross_imag], 0)
    solution = jnp.linalg.solve(system, right_side)
    mixing_real = solution[:BANDS]
    mixing_imag = solution[BANDS:]
    block_real = band_block[:, :, 0]
    block_imag = band_block[:, :, 1]
    combine = lambda data, mixing: jnp.einsum('iabcd,ij->jabcd', data, mixing, precision=HIGHEST)
    residual_real = image[:, :, 0] - (combine(block_real, mixing_real) - combine(block_imag, mixing_imag))
    residual_imag = image[:, :, 1] - (combine(block_real, mixing_imag) + combine(block_imag, mixing_real))
    search_block = jnp.stack([residual_real, residual_imag], axis=2) / (magnitude * magnitude + 1.0)
    search_image = operate(search_block, inverse_cells, primary, secondary, magnitude)
    stacked = jnp.concatenate([band_block, search_block], 0)
    images = jnp.concatenate([image, search_image], 0)
    full_real, full_imag = gram_parts(stacked, stacked)
    proj_real, proj_imag = gram_parts(stacked, images)
    return (search_block, jnp.stack([full_real, full_imag], 0), jnp.stack([proj_real, proj_imag], 0))
```

```python
from functools import partial
import math

import jax
import jax.numpy as jnp
from jax import lax
from jax.experimental import pallas as pl
from jax.experimental.pallas import tpu as pltpu
from jax.sharding import PartitionSpec as P

KPOINTS = 8


HIGHEST = lax.Precision.HIGHEST


def axis_values(length, weight, fraction, offset, extent):
    indices = offset + jnp.arange(extent, dtype=jnp.int32)
    signed = jnp.where(indices >= length // 2, indices - length, indices).astype(jnp.float32)
    return 2.0 * math.pi / length * (signed + weight * fraction)


def frame(depth_wave, height_wave, width_wave):
    depth_term = depth_wave[:, None, None]
    height_term = height_wave[None, :, None]
    width_term = width_wave[None, None, :]
    planar = jnp.sqrt(width_term * width_term + height_term * height_term)
    magnitude = jnp.sqrt(planar * planar + depth_term * depth_term)
    grid_shape = magnitude.shape
    primary = [
        jnp.broadcast_to(height_term / planar, grid_shape),
        jnp.broadcast_to(-width_term / planar, grid_shape),
        jnp.zeros(grid_shape, magnitude.dtype),
    ]
    secondary = [
        width_term * depth_term / (magnitude * planar),
        height_term * depth_term / (magnitude * planar),
        -planar / magnitude,
    ]
    return (primary, secondary, magnitude)


def curl_field(block, primary, secondary, magnitude):
    first_comp = block[:, 0]
    second_comp = block[:, 1]
    parts = [
        magnitude * (first_comp * secondary[component] - second_comp * primary[component])
        for component in range(3)
    ]
    return jnp.stack(parts, axis=1).reshape((-1,) + first_comp.shape[1:])


def project_back(spectrum, primary, secondary, magnitude, band_count):
    grouped = spectrum.reshape((band_count, 3) + spectrum.shape[1:])
    along_second = (
        grouped[:, 0] * secondary[0] + grouped[:, 1] * secondary[1] + grouped[:, 2] * secondary[2]
    )
    along_primary = (
        grouped[:, 0] * primary[0] + grouped[:, 1] * primary[1] + grouped[:, 2] * primary[2]
    )
    return jnp.stack([magnitude * along_second, -magnitude * along_primary], axis=1)


def transform(values, target, direction):
    length = values.shape[target]
    indices = jnp.arange(length, dtype=jnp.int32)
    products = indices[:, None] * indices[None, :] % length
    angles = 2.0 * math.pi / length * products.astype(jnp.float32)
    cosine = jnp.cos(angles)
    sine_table = direction * jnp.sin(angles)
    letters = "abc"
    source = letters[target - 2]
    formula = "i" + letters + "," + source + "w" + "->" + "i" + letters.replace(source, "w")
    contract = partial(jnp.einsum, formula, precision=HIGHEST)
    real_part = values[:, 0]
    imaginary = values[:, 1]
    new_real = contract(real_part, cosine) - contract(imaginary, sine_table)
    new_imag = contract(real_part, sine_table) + contract(imaginary, cosine)
    return jnp.stack([new_real, new_imag], axis=1)


def cell_values(material_grid, inverse_permittivity, grid_cells):
    inverse_cells = jnp.zeros(material_grid.shape, jnp.float32)
    for material in range(inverse_permittivity.shape[0]):
        inverse_cells = inverse_cells + jnp.where(
            material_grid == material, inverse_permittivity[material], 0.0
        )
    return inverse_cells / grid_cells


def depth_step(shape):
    depth = shape[3]
    step = depth
    plane = 4 * math.prod(shape[:3]) * math.prod(shape[4:])
    while step % 2 == 0 and step * plane > (1 << 20):
        step //= 2
    return step


def block_spec(shape, step):
    return pl.BlockSpec(shape[:3] + (step,) + shape[4:], lambda d: (0, 0, 0, d, 0, 0))


def gram_kernel(plan, step, *refs):
    *inputs, out = refs
    rows, lanes = inputs[0].shape[4:]

    @pl.when(pl.program_id(0) == 0)
    def _():
        out[...] = jnp.zeros_like(out)

    base = 0
    for (left, left_band), rights in plan:

        def body(depth, sums, left=left, left_band=left_band, rights=rights):
            sums = list(sums)
            for row in range(0, rows, 8):
                for lane in range(0, lanes, 128):
                    tile = (depth, pl.ds(row, 8), pl.ds(lane, 128))
                    for comp in range(2):
                        left_real = inputs[left][(left_band, comp, 0) + tile]
                        left_imag = inputs[left][(left_band, comp, 1) + tile]
                        for place, (right, right_band) in enumerate(rights):
                            right_real = inputs[right][(right_band, comp, 0) + tile]
                            right_imag = inputs[right][(right_band, comp, 1) + tile]
                            sums[2 * place] += left_real * right_real + left_imag * right_imag
                            sums[2 * place + 1] += left_real * right_imag - left_imag * right_real
            return tuple(sums)

        zeros = tuple(jnp.zeros((8, 128), jnp.float32) for _ in range(2 * len(rights)))
        sums = lax.fori_loop(0, step, body, zeros)
        for place, value in enumerate(sums):
            out[base + place] += value
        base += 2 * len(rights)


def gram_sums(arrays, pairs):
    shape = arrays[0].shape
    bands = shape[0]
    step = depth_step(shape)
    plan = []
    for left in sorted({left for left, _ in pairs}):
        for band in range(bands):
            rights = [(r, j) for l, r in pairs if l == left for j in range(bands)]
            plan.append(((left, band), rights))
    count = sum(2 * len(rights) for _, rights in plan)
    cells = math.prod(shape[3:])
    sums = pl.pallas_call(
        partial(gram_kernel, plan, step),
        grid=(shape[3] // step,),
        in_specs=[block_spec(shape, step) for _ in arrays],
        out_specs=pl.BlockSpec((count, 8, 128), lambda d: (0, 0, 0)),
        out_shape=jax.ShapeDtypeStruct((count, 8, 128), jnp.float32),
        cost_estimate=pl.CostEstimate(
            flops=8 * count * cells,
            bytes_accessed=4 * len(arrays) * math.prod(shape),
            transcendentals=0,
        ),
    )(*arrays)
    sums = jnp.sum(sums, axis=(1, 2))
    order = []
    for left in sorted({left for left, _ in pairs}):
        order.append([p for p in pairs if p[0] == left])
    found = {}
    base = 0
    for group in order:
        size = bands * len(group) * bands * 2
        part = sums[base : base + size].reshape(bands, len(group), bands, 2)
        for place, pair in enumerate(group):
            found[pair] = part[:, place]
        base += size
    return [found[pair] for pair in pairs]


def residual_kernel(mixing, block, image, weight, out):
    bands, _, _, step, rows, lanes = block.shape

    @pl.loop(0, step)
    def _(depth):
        for row in range(0, rows, 8):
            for lane in range(0, lanes, 128):
                tile = (depth, pl.ds(row, 8), pl.ds(lane, 128))
                scale = weight[tile]
                for comp in range(2):
                    reals = [block[(i, comp, 0) + tile] for i in range(bands)]
                    imags = [block[(i, comp, 1) + tile] for i in range(bands)]
                    for j in range(bands):
                        real = reals[0] * mixing[0, j] - imags[0] * mixing[bands, j]
                        imag = reals[0] * mixing[bands, j] + imags[0] * mixing[0, j]
                        for i in range(1, bands):
                            real += reals[i] * mixing[i, j] - imags[i] * mixing[bands + i, j]
                            imag += reals[i] * mixing[bands + i, j] + imags[i] * mixing[i, j]
                        out[(j, comp, 0) + tile] = (image[(j, comp, 0) + tile] - real) / scale
                        out[(j, comp, 1) + tile] = (image[(j, comp, 1) + tile] - imag) / scale


def residual_block(block, image, mixing, weight):
    shape = block.shape
    step = depth_step(shape)
    spec = block_spec(shape, step)
    return pl.pallas_call(
        residual_kernel,
        grid=(shape[3] // step,),
        in_specs=[
            pl.BlockSpec(memory_space=pltpu.SMEM),
            spec,
            spec,
            pl.BlockSpec((step,) + shape[4:], lambda d: (d, 0, 0)),
        ],
        out_specs=spec,
        out_shape=jax.ShapeDtypeStruct(shape, jnp.float32),
    )(mixing, block, image, weight)


def sum_over_devices(values):
    flat = jnp.concatenate([value.reshape(-1) for value in values])
    for axis in ("slab", "band"):
        flat = jnp.sum(lax.all_gather(flat, axis), axis=0)
    totals = []
    base = 0
    for value in values:
        totals.append(flat[base : base + value.size].reshape(value.shape))
        base += value.size
    return totals


def shards(band_block, material_grid, inverse_permittivity, bloch_index):
    band_groups = lax.axis_size("band")
    slab_count = lax.axis_size("slab")
    band_count = band_block.shape[0]
    depth_share = band_block.shape[3]
    row_share = band_block.shape[4]
    line_length = band_block.shape[5]
    full_depth = depth_share * band_groups
    full_rows = row_share * slab_count
    grid_cells = full_depth * full_rows * line_length
    fraction = (bloch_index[0].astype(jnp.float32) + 1.0) / KPOINTS
    row_offset = lax.axis_index("slab") * row_share
    depth_offset = lax.axis_index("band") * depth_share
    width_wave = axis_values(line_length, 0.5, fraction, 0, line_length)
    row_wave = axis_values(full_rows, 0.35, fraction, row_offset, row_share)
    point_frame = frame(
        axis_values(full_depth, 0.2, fraction, depth_offset, depth_share), row_wave, width_wave
    )
    inverse_cells = cell_values(material_grid, inverse_permittivity, grid_cells)

    def slab_operator(points):
        gathered = lax.all_to_all(points, "band", split_axis=0, concat_axis=3, tiled=True)
        primary, secondary, magnitude = frame(
            axis_values(full_depth, 0.2, fraction, 0, full_depth), row_wave, width_wave
        )
        curled = curl_field(gathered, primary, secondary, magnitude)
        spectrum = transform(transform(curled, 4, 1.0), 2, 1.0)
        spatial = (
            transform(
                lax.all_to_all(spectrum, "slab", split_axis=2, concat_axis=3, tiled=True), 3, 1.0
            )
            * inverse_cells[None, None]
        )
        returned = lax.all_to_all(
            transform(spatial, 3, -1.0), "slab", split_axis=3, concat_axis=2, tiled=True
        )
        finished = transform(transform(returned, 2, -1.0), 4, -1.0)
        local_image = project_back(finished, primary, secondary, magnitude, gathered.shape[0])
        return lax.all_to_all(local_image, "band", split_axis=3, concat_axis=0, tiled=True)

    def apply_operator(points):
        return slab_operator(points)

    image = apply_operator(band_block)
    (own_sum,) = gram_sums([band_block], [(0, 0)])
    (cross_sum,) = gram_sums([band_block, image], [(0, 1)])
    own_total, cross_total = sum_over_devices([own_sum, cross_sum])
    correlation_real = own_total[..., 0] / grid_cells
    correlation_imag = own_total[..., 1] / grid_cells
    cross_real = cross_total[..., 0] / grid_cells
    cross_imag = cross_total[..., 1] / grid_cells
    system = jnp.concatenate(
        [
            jnp.concatenate([correlation_real, -correlation_imag], 1),
            jnp.concatenate([correlation_imag, correlation_real], 1),
        ],
        0,
    )
    right_side = jnp.concatenate([cross_real, cross_imag], 0)
    factor = jnp.linalg.cholesky(system)
    solution = jax.scipy.linalg.cho_solve((factor, True), right_side)
    magnitude = point_frame[2]
    search_block = residual_block(band_block, image, solution, magnitude * magnitude + 1.0)
    search_image = apply_operator(search_block)
    early = gram_sums([band_block, search_block, image], [(0, 1), (1, 1), (1, 2)])
    late = gram_sums([band_block, search_block, search_image], [(0, 2), (1, 2)])
    totals = [total / grid_cells for total in sum_over_devices(early + late)]
    joint = jnp.concatenate(totals[:2], 0)
    across = jnp.concatenate(totals[3:], 0)
    joint_real, joint_imag = joint[..., 0], joint[..., 1]
    back_real, back_imag = totals[2][..., 0], totals[2][..., 1]
    image_real, image_imag = across[..., 0], across[..., 1]
    upper_real = jnp.concatenate([correlation_real, joint_real[:band_count]], 1)
    lower_real = jnp.concatenate([joint_real[:band_count].T, joint_real[band_count:]], 1)
    upper_imag = jnp.concatenate([correlation_imag, joint_imag[:band_count]], 1)
    lower_imag = jnp.concatenate([-joint_imag[:band_count].T, joint_imag[band_count:]], 1)
    correlation = jnp.stack(
        [
            jnp.concatenate([upper_real, lower_real], 0),
            jnp.concatenate([upper_imag, lower_imag], 0),
        ],
        0,
    )
    top_real = jnp.concatenate([cross_real, image_real[:band_count]], 1)
    bottom_real = jnp.concatenate([back_real, image_real[band_count:]], 1)
    top_imag = jnp.concatenate([cross_imag, image_imag[:band_count]], 1)
    bottom_imag = jnp.concatenate([back_imag, image_imag[band_count:]], 1)
    projected = jnp.stack(
        [jnp.concatenate([top_real, bottom_real], 0), jnp.concatenate([top_imag, bottom_imag], 0)],
        0,
    )
    return (search_block, correlation, projected)


def solution(mesh):
    return jax.shard_map(
        shards,
        mesh=mesh,
        in_specs=(P(None, None, None, "band", "slab", None), P("slab", None, None), P(), P()),
        out_specs=(P(None, None, None, "band", "slab", None), P(), P()),
        check_vma=False,
    )
```
